32 devices in a mesh: table: 8 (over z, x), replica: 4 (over y, core).
Axes of the slice: x: 2, y: 2, z: 4, core: 2. Of those that a mesh axis runs over, the one named last changes fastest.
Arguments:
- emb_table: bfloat16 [8192, 128], P('table'), may hold values from -3 to 3
- cross_up: bfloat16 [256, 3456], replicated, may hold values from -0.375 to 0.375
- cross_down: bfloat16 [256, 3456], replicated, may hold values from -0.109375 to 0.109375
- cross_bias: float32 [3456], replicated, may hold values from -3 to 3
- out_weight: float32 [3456], replicated, may hold values from -0.109375 to 0.109375
- bottom_weight: float32 [13, 128], replicated, may hold values from -1.75 to 1.75
- bottom_bias: float32 [128], replicated, may hold values from -3 to 3
- dense_in: float32 [4096, 13], P(('table', 'replica')), may hold values from -6 to 6
- labels: int32 [4096], P(('table', 'replica')), may hold values from 0 to 1
- lookup_ids: int32 [4096, 26, 4], P(('table', 'replica')), may hold values from 0 to 767
- bag_weight: float32 [4096, 26, 4], P(('table', 'replica')), may hold values from 0.25 to 1
- bag_length: int32 [4096, 26], P(('table', 'replica')), may hold values from 1 to 4
- want_blocks: int32 [8, 4, 8, 1], P('table', 'replica'), may hold values from 0 to 31
- hot_blocks: int32 [8, 2], P('table'), may hold values from 0 to 31
- hot_count: int32 [8], P('table'), may hold values from 1 to 2, as said below
Outputs:
- up_grad: float32 [256, 3456], P(('table', 'replica'))
- down_grad: float32 [256, 3456], P(('table', 'replica'))
- table_grad: float32 [8192, 128], P(('table', 'replica'))
The draws below stay inside these ranges and needn't reach their ends.
Inputs may be any that keep to these rules, and one draw needn't show every extreme that they name: `hot_count`: each owner has 1 to 2 live hot slots, and some owner has 2.
All inputs are finite; a program needn't handle non-finite values.
Results may differ from the reference program's by a relative error of at most 0.0053.
Values may be sent and summed in bfloat16 or wider, within the bound.
A program may use at most 64 MiB of HBM per device.

```python
import jax
import jax.numpy as jnp
from jax import lax

EMB = 128
FEATS = 26
DENSE = 13
RANK = 256
BLOCK = 32
BAG = 4
WANT = 1
HOT_MOST = 2
B_DEV = 128
BLOCKS_DEV = 32
OWNERS = 8
ROWS = 8192
CACHE = 768
DI = 3456
SAMPLES = 4096
N_TABLE = 8
N_REPLICA = 4


def draw_hot_count(key, part):
    first_key, second_key = jax.random.split(jax.random.fold_in(key, 7))
    doubled = (jax.random.randint(first_key, (OWNERS,), 0, 4) == 0).astype(jnp.int32) * (HOT_MOST - 1)
    chosen = jax.random.randint(second_key, (), 0, OWNERS)
    return jnp.where(jnp.arange(OWNERS) == chosen, HOT_MOST, 1 + doubled).astype(jnp.int32)


def with_ends(entries, rng, least, high):
    longest = entries.shape.index(max(entries.shape))
    spots = []
    for shift in (0, 1):
        where = [jax.random.randint(jax.random.fold_in(rng, axis), (), 0, length) for axis, length in enumerate(entries.shape)]
        where[longest] = (where[longest] + shift) % entries.shape[longest]
        spots.append(tuple(where))
    return entries.at[spots[0]].set(least).at[spots[1]].set(high)


def shard_levels(own_key, dims, cuts, low, largest):
    gain = 1.0
    for axis_at, shards_of in cuts:
        steps = jax.random.uniform(jax.random.fold_in(jax.random.fold_in(own_key, 6), axis_at), (shards_of,), jnp.float32, low / len(cuts), largest / len(cuts))
        gain = gain * jnp.repeat(jnp.exp(steps), dims[axis_at] // shards_of).reshape((-1,) + (1,) * (len(dims) - 1 - axis_at))
    return gain


def gaussian(rng, shape, scale, bound, pieces=(), kind=jnp.bfloat16):
    result = scale * jax.random.normal(rng, shape, jnp.float32)
    if pieces:
        result = result * shard_levels(rng, shape, pieces, -0.22, 0.18)
    return jnp.clip(result, -bound, bound).astype(kind)


def setup_inputs(seed: int = 0) -> dict:
    streams_of = jax.random.split(jax.random.key(seed), 16)
    return {
        "emb_table": gaussian(streams_of[0], (ROWS, EMB), 0.5, 3.0, ((0, 8),)),
        "cross_up": gaussian(streams_of[1], (RANK, DI), RANK ** -0.5, 0.375),
        "cross_down": gaussian(streams_of[2], (RANK, DI), DI ** -0.5, 0.109375),
        "cross_bias": gaussian(streams_of[3], (DI,), 0.5, 3.0, (), jnp.float32),
        "out_weight": gaussian(streams_of[4], (DI,), DI ** -0.5, 0.109375, (), jnp.float32),
        "bottom_weight": gaussian(streams_of[5], (DENSE, EMB), DENSE ** -0.5, 1.75, (), jnp.float32),
        "bottom_bias": gaussian(streams_of[6], (EMB,), 0.5, 3.0, (), jnp.float32),
        "dense_in": gaussian(streams_of[7], (SAMPLES, DENSE), 1.0, 6.0, ((0, 32),), jnp.float32),
        "labels": with_ends(jax.random.randint(streams_of[8], (SAMPLES,), 0, 2), jax.random.fold_in(streams_of[8], 1), 0, 1).astype(jnp.int32),
        "lookup_ids": with_ends(jax.random.randint(streams_of[9], (SAMPLES, FEATS, BAG), 0, CACHE), jax.random.fold_in(streams_of[9], 1), 0, CACHE - 1).astype(jnp.int32),
        "bag_weight": jnp.clip(0.25 + 0.75 * jax.random.uniform(streams_of[10], (SAMPLES, FEATS, BAG), jnp.float32) ** shard_levels(streams_of[10], (SAMPLES, FEATS, BAG), ((0, 32),), -0.2, 0.2), 0.25, 1.0),
        "bag_length": with_ends(jax.random.randint(streams_of[11], (SAMPLES, FEATS), 1, BAG + 1), jax.random.fold_in(streams_of[11], 1), 1, BAG).astype(jnp.int32),
        "want_blocks": with_ends(jax.random.randint(streams_of[12], (OWNERS, N_REPLICA, OWNERS, WANT), 0, BLOCKS_DEV), jax.random.fold_in(streams_of[12], 1), 0, BLOCKS_DEV - 1).astype(jnp.int32),
        "hot_blocks": with_ends(jax.random.randint(streams_of[13], (OWNERS, HOT_MOST), 0, BLOCKS_DEV), jax.random.fold_in(streams_of[13], 1), 0, BLOCKS_DEV - 1).astype(jnp.int32),
        "hot_count": draw_hot_count(jax.random.fold_in(streams_of[15], 71), 0),
    }


def local_step(cached_rows, dense_dev, labels_dev, ids_dev, weight_dev, length_dev, cross_up, cross_down, cross_bias, out_weight, bottom_weight, bottom_bias):
    batch = ids_dev.shape[0]
    width = cached_rows.shape[1]
    gathered = cached_rows[ids_dev].astype(jnp.float32)
    slots = jnp.arange(ids_dev.shape[2], dtype=jnp.int32)
    bag_coef = jnp.where(slots[None, None, :] < length_dev[:, :, None], weight_dev, jnp.zeros((), jnp.float32))
    pooled = jnp.sum(bag_coef[..., None] * gathered, axis=2)
    bottom = jax.nn.relu(jnp.dot(dense_dev, bottom_weight, precision=lax.Precision.HIGHEST) + bottom_bias)
    cross_base = jnp.concatenate([bottom, pooled.reshape(batch, -1)], 1).astype(jnp.bfloat16)
    low_rank = lax.dot_general(cross_base, cross_down, (((1,), (1,)), ((), ())), preferred_element_type=jnp.float32).astype(jnp.bfloat16)
    cross_gate = jnp.dot(low_rank, cross_up, preferred_element_type=jnp.float32) + cross_bias
    base_wide = cross_base.astype(jnp.float32)
    crossed = base_wide * cross_gate + base_wide
    logits = jnp.dot(crossed, out_weight, precision=lax.Precision.HIGHEST)
    logit_grad = jax.nn.sigmoid(logits) - labels_dev.astype(jnp.float32)
    grad_crossed = logit_grad[:, None] * out_weight[None, :]
    g_cross = (grad_crossed * base_wide).astype(jnp.bfloat16)
    g_low = lax.dot_general(g_cross, cross_up, (((1,), (1,)), ((), ())), preferred_element_type=jnp.float32).astype(jnp.bfloat16)
    up_part = lax.dot_general(low_rank, g_cross, (((0,), (0,)), ((), ())), preferred_element_type=jnp.float32)
    down_part = lax.dot_general(g_low, cross_base, (((0,), (0,)), ((), ())), preferred_element_type=jnp.float32)
    grad_base = grad_crossed * (cross_gate + 1.0) + jnp.dot(g_low, cross_down, preferred_element_type=jnp.float32)
    grad_pooled = grad_base[:, width:].reshape(batch, -1, width)
    contrib = bag_coef[..., None] * grad_pooled[:, :, None, :]
    cache_grad = jnp.zeros(cached_rows.shape, jnp.float32).at[ids_dev.reshape(-1)].add(contrib.reshape(-1, width))
    return up_part, down_part, cache_grad


def reference(emb_table, cross_up, cross_down, cross_bias, out_weight, bottom_weight, bottom_bias, dense_in, labels, lookup_ids, bag_weight, bag_length, want_blocks, hot_blocks, hot_count):
    devices_all = N_TABLE * N_REPLICA
    blocks = emb_table.reshape(OWNERS, BLOCKS_DEV, BLOCK, EMB)
    owner_ids = jnp.arange(OWNERS, dtype=jnp.int32)
    alive = jnp.arange(HOT_MOST, dtype=jnp.int32)[:, None] < hot_count[None, :]
    hot_rows = jnp.where(alive[:, :, None, None], blocks[owner_ids[None, :], hot_blocks.T], jnp.zeros((), jnp.bfloat16))
    hot_flat = hot_rows.reshape(-1, EMB)
    cold_count = OWNERS * WANT * BLOCK
    wanted = want_blocks.reshape(devices_all, OWNERS, WANT)
    items = (wanted,
             dense_in.reshape(devices_all, B_DEV, DENSE),
             labels.reshape(devices_all, B_DEV),
             lookup_ids.reshape(devices_all, B_DEV, FEATS, BAG),
             bag_weight.reshape(devices_all, B_DEV, FEATS, BAG),
             bag_length.reshape(devices_all, B_DEV, FEATS))

    def device_turn(running, device_item):
        block_grad, hot_grad, up_sum, down_sum = running
        wanted_dev, dense_dev, labels_dev, ids_dev, weight_dev, length_dev = device_item
        cold_rows = blocks[owner_ids[:, None], wanted_dev]
        cached_rows = jnp.concatenate([cold_rows.reshape(-1, EMB), hot_flat], 0)
        up_part, down_part, cache_grad = local_step(cached_rows, dense_dev, labels_dev, ids_dev, weight_dev, length_dev, cross_up, cross_down, cross_bias, out_weight, bottom_weight, bottom_bias)
        cold_grad = lax.optimization_barrier(cache_grad[:cold_count].astype(jnp.bfloat16)).astype(jnp.float32)
        block_grad = block_grad.at[owner_ids[:, None], wanted_dev].add(cold_grad.reshape(OWNERS, WANT, BLOCK, EMB))
        hot_grad = hot_grad + cache_grad[cold_count:]
        return (block_grad, hot_grad, up_sum + up_part, down_sum + down_part), None

    start = (jnp.zeros((OWNERS, BLOCKS_DEV, BLOCK, EMB), jnp.float32),
             jnp.zeros((HOT_MOST * OWNERS * BLOCK, EMB), jnp.float32),
             jnp.zeros((RANK, DI), jnp.float32),
             jnp.zeros((RANK, DI), jnp.float32))
    (block_grad, hot_grad, up_sum, down_sum), _ = lax.scan(device_turn, start, items)
    hot_sums = jnp.where(alive[:, :, None, None], hot_grad.reshape(HOT_MOST, OWNERS, BLOCK, EMB), jnp.zeros((), jnp.float32))
    block_grad = block_grad.at[owner_ids[None, :], hot_blocks.T].add(hot_sums)
    return up_sum, down_sum, block_grad.reshape(ROWS, EMB)
```

```python
import functools

import jax
import jax.numpy as jnp
from jax import lax
from jax.experimental import pallas as pl
from jax.experimental.pallas import tpu as pltpu
from jax.sharding import PartitionSpec as P

EMB = 128
BLOCK = 32
LANES = 128
SUBLANES = 8
MESH = pl.DeviceIdType.MESH
F32 = jnp.float32
BF16 = jnp.bfloat16


def vmem(n):
    return [pl.BlockSpec(memory_space=pltpu.VMEM)] * n


def pick_rows(ids, emb_ref):
    total = emb_ref.shape[0]
    tiles = total // LANES
    row = lax.broadcasted_iota(jnp.int32, (BLOCK, LANES), 0)
    lane = lax.broadcasted_iota(jnp.int32, (BLOCK, LANES), 1)
    parts = []
    for block in ids:
        want = block * BLOCK + row
        parts.append(
            jnp.concatenate(
                [jnp.where(want == lane + LANES * c, 1.0, 0.0) for c in range(tiles)], axis=1
            )
        )
    pick = jnp.concatenate(parts, axis=0).astype(BF16)
    return jnp.dot(pick, emb_ref[...], preferred_element_type=F32).astype(BF16)


def fetch_kernel(
    owners, want_ref, hot_ref, emb_ref, cold_ref, hot_out, ask_ref, serve, own_hot,
    id_send, id_recv, hs_send, hs_recv, cs_send, cs_recv,
):
    me = lax.axis_index("table")
    slots = hot_ref.shape[0]
    wants = want_ref.shape[1]

    def peer(k):
        return lax.rem(me + k, owners)

    def copy(src, dst, send, recv, k):
        return pltpu.make_async_remote_copy(
            src_ref=src, dst_ref=dst, send_sem=send.at[k], recv_sem=recv.at[k],
            device_id=(peer(k), lax.axis_index("replica")), device_id_type=MESH,
        )

    barrier = pltpu.get_barrier_semaphore()
    for k in range(1, owners):
        pl.semaphore_signal(
            barrier, inc=1, device_id=(peer(k), lax.axis_index("replica")), device_id_type=MESH
        )
    ask_ref[me] = want_ref[me]
    hot = pick_rows([hot_ref[s, 0:1, :] for s in range(slots)], emb_ref)
    hot = hot.reshape(slots, BLOCK, EMB)
    own_hot[...] = hot
    hot_out[:, me] = hot
    pl.semaphore_wait(barrier, owners - 1)

    id_copies = [
        copy(want_ref.at[peer(k)], ask_ref.at[me], id_send, id_recv, k) for k in range(1, owners)
    ]
    for c in id_copies:
        c.start()
    hot_copies = [
        copy(own_hot, hot_out.at[:, me], hs_send, hs_recv, k) for k in range(1, owners)
    ]
    for c in hot_copies:
        c.start()
    for c in id_copies:
        c.wait()
    asked = [ask_ref[p, w, 0:1, :] for p in range(owners) for w in range(wants)]
    serve[...] = pick_rows(asked, emb_ref).reshape(owners, wants, BLOCK, EMB)
    cold_copies = [
        copy(serve.at[peer(k)], cold_ref.at[me], cs_send, cs_recv, k) for k in range(1, owners)
    ]
    for c in cold_copies:
        c.start()
    cold_ref[me] = serve[me]
    for c in hot_copies + cold_copies:
        c.wait()


def fetch(want, hot_ids, emb, owners):
    wants, slots = want.shape[1], hot_ids.shape[0]
    sems = [pltpu.SemaphoreType.DMA((owners,))] * 6
    return pl.pallas_call(
        functools.partial(fetch_kernel, owners),
        out_shape=[
            jax.ShapeDtypeStruct((owners, wants, BLOCK, EMB), BF16),
            jax.ShapeDtypeStruct((slots, owners, BLOCK, EMB), BF16),
            jax.ShapeDtypeStruct(want.shape, jnp.int32),
        ],
        in_specs=vmem(3),
        out_specs=vmem(3),
        scratch_shapes=[
            pltpu.VMEM((owners, wants, BLOCK, EMB), BF16),
            pltpu.VMEM((slots, BLOCK, EMB), BF16),
        ] + sems,
        compiler_params=pltpu.CompilerParams(collective_id=0, has_side_effects=True),
        name="fetch",
    )(want, hot_ids, emb)


def compute_kernel(
    plan, bag,
    cold_ref, hot_ref, ids_ref, weight_ref, length_ref, dense_ref, label_ref, up_ref, down_ref, bias_ref,
    outw_ref, bw_ref, bb_ref,
    acc_ref, cold_grad, hot_grad,
    pick, rows, base, gate, gcross, grad, ids_cols, coef_cols, turn,
):
    feats, batch, cache = pick.shape
    cold = cold_ref.shape[0]
    width = base.shape[1]
    group = 16
    rows[:cold] = cold_ref[...]
    rows[cold:] = hot_ref[...]

    turn[...] = jnp.zeros_like(turn)
    for f in range(feats):
        turn[f * bag:(f + 1) * bag, :] = ids_ref[f].astype(F32)
    ids_cols[...] = turn[...].T
    spot = lax.broadcasted_iota(jnp.int32, (bag, batch), 0)
    for f in range(feats):
        live = spot < length_ref[f:f + 1, :]
        turn[f * bag:(f + 1) * bag, :] = jnp.where(live, weight_ref[f], 0.0)
    coef_cols[...] = turn[...].T

    @pl.loop(0, batch // group)
    def _(g):
        at = pl.ds(pl.multiple_of(g * group, group), group)
        ids = ids_cols[at, :]
        coef = coef_cols[at, :]
        lane = lax.broadcasted_iota(jnp.int32, (group, cache), 1).astype(F32)
        for f in range(feats):
            total = None
            for l in range(bag):
                j = f * bag + l
                term = jnp.where(ids[:, j:j + 1] == lane, coef[:, j:j + 1], 0.0)
                total = term if total is None else total + term
            pick[f, at, :] = total.astype(BF16)

    bottom = jnp.zeros((batch, EMB), F32) + bb_ref[...]
    features = dense_ref.shape[0]
    turn[0:features, :] = dense_ref[...]
    turn[features:features + 1, :] = label_ref[...].astype(F32)
    dense = turn[...].T
    label = dense[:, features:features + 1]
    for j in range(features):
        bottom = bottom + dense[:, j:j + 1] * bw_ref[j:j + 1, :]
    base[:, 0:EMB] = jnp.maximum(bottom, 0.0).astype(BF16)

    @pl.loop(0, feats)
    def _(f):
        at = pl.ds(pl.multiple_of((f + 1) * EMB, EMB), EMB)
        base[:, at] = jnp.dot(pick[f], rows[...], preferred_element_type=F32).astype(BF16)

    nt = (((1,), (1,)), ((), ()))
    low_wide = lax.dot_general(base[...], down_ref[...], nt, preferred_element_type=F32)
    low = low_wide.astype(BF16)
    low_t = low.astype(F32).T.astype(BF16)
    step = width // len(plan)
    lsum = jnp.zeros((batch, LANES), F32)
    for c in range(width // step):
        at = slice(c * step, (c + 1) * step)
        g = jnp.dot(low, up_ref[:, at], preferred_element_type=F32) + bias_ref[:, at]
        gate[:, at] = g
        b = base[:, at].astype(F32)
        x = (b * g + b) * outw_ref[:, at]
        for i in range(step // LANES):
            lsum = lsum + x[:, i * LANES:(i + 1) * LANES]
    logit = jnp.sum(lsum, axis=1, keepdims=True)
    lgrad = jax.nn.sigmoid(logit) - label

    for c in range(width // step):
        at = slice(c * step, (c + 1) * step)
        gc = lgrad * outw_ref[:, at]
        gcross[:, at] = (gc * base[:, at].astype(F32)).astype(BF16)
    g_low = lax.dot_general(gcross[...], up_ref[...], nt, preferred_element_type=F32)
    g_low = g_low.astype(BF16)
    g_low_t = g_low.astype(F32).T.astype(BF16)
    devices, two = acc_ref.shape[0], acc_ref.shape[1]
    half = two // 2
    for c, place in enumerate(plan):
        at = slice(c * step, (c + 1) * step)
        up = jnp.dot(low_t, gcross[:, at], preferred_element_type=F32)
        down = jnp.dot(g_low_t, base[:, at], preferred_element_type=F32)
        for d in range(devices):
            acc_ref[place[d], 0:half, at] = up[d * half:(d + 1) * half, :]
            acc_ref[place[d], half:two, at] = down[d * half:(d + 1) * half, :]
        gc = lgrad * outw_ref[:, at]
        grad[:, at] = gc * (gate[:, at] + 1.0) + jnp.dot(
            g_low, down_ref[:, at], preferred_element_type=F32
        )

    total = jnp.zeros((EMB, cache), F32)
    for f in range(feats):
        gp = grad[:, (f + 1) * EMB:(f + 2) * EMB].T.astype(BF16)
        total = total + jnp.dot(gp, pick[f], preferred_element_type=F32)
    total = total.T
    cold_grad[...] = total[:cold].astype(BF16)
    hot_grad[...] = total[cold:].astype(BF16)


def compute(plan, devices, cold, hot, ids, weight, length, dense, labels, up, down, bias, outw, bw, bb):
    feats, bag, batch = ids.shape
    padded = -(-feats * bag // LANES) * LANES
    width = up.shape[1]
    cache = cold.shape[0] + hot.shape[0]
    share = up.shape[0] // devices
    return pl.pallas_call(
        functools.partial(compute_kernel, plan, bag),
        out_shape=[
            jax.ShapeDtypeStruct((devices, 2 * share, width), F32),
            jax.ShapeDtypeStruct(cold.shape, BF16),
            jax.ShapeDtypeStruct(hot.shape, BF16),
        ],
        in_specs=vmem(13),
        out_specs=vmem(3),
        scratch_shapes=[
            pltpu.VMEM((feats, batch, cache), BF16),
            pltpu.VMEM((cache, EMB), BF16),
            pltpu.VMEM((batch, width), BF16),
            pltpu.VMEM((batch, width), F32),
            pltpu.VMEM((batch, width), BF16),
            pltpu.VMEM((batch, width), F32),
            pltpu.VMEM((batch, padded), F32),
            pltpu.VMEM((batch, padded), F32),
            pltpu.VMEM((padded, batch), F32),
        ],
        name="compute",
    )(cold, hot, ids, weight, length, dense, labels, up, down, bias, outw, bw, bb)


def reduce_kernel(
    stages, n_table, n_rep, buffers,
    acc_in, tg_cold, tg_hot, ask_ref, hot_ref,
    up_out, down_out, table_out,
    acc, rc_cold, rc_hot, own_cold, own_hot, ag_cold, ag_hot, own_ids, ag_ids,
    *rest,
):
    sends = rest[:buffers]
    recvs = rest[buffers:2 * buffers]
    w_send, w_recv, c_send, c_recv, h_send, h_recv, a_send, a_recv = rest[2 * buffers:]
    t = lax.axis_index("table")
    r = lax.axis_index("replica")
    parts = len(stages)
    step = acc.shape[2] // parts

    def table_peer(k):
        return (lax.rem(t + k, n_table), r)

    def rep_peer(k):
        return (t, lax.rem(r + k, n_rep))

    barrier = pltpu.get_barrier_semaphore()
    for k in range(1, n_table):
        pl.semaphore_signal(barrier, inc=1, device_id=table_peer(k), device_id_type=MESH)
    for k in range(1, n_rep):
        pl.semaphore_signal(barrier, inc=1, device_id=rep_peer(k), device_id_type=MESH)
    pl.semaphore_wait(barrier, n_table - 1 + n_rep - 1)

    def bit_of(axis, bit):
        return lax.rem((t if axis == "table" else r) // (1 << bit), 2)

    def partner(axis, bit):
        mine = bit_of(axis, bit)
        shift = (1 - 2 * mine) * (1 << bit)
        return (t + shift, r) if axis == "table" else (t, r + shift)

    lows = [0] * parts
    sizes = [acc.shape[0]] * parts
    copies = {}

    def launch(p, s):
        axis, bit = stages[p][s]
        mine = bit_of(axis, bit)
        half = sizes[p] // 2
        keep = lows[p] + mine * half
        give = lows[p] + (1 - mine) * half
        cols = slice(p * step, (p + 1) * step)
        i = p * len(stages[p]) + s
        src = acc_in if s == 0 else acc
        sends[i][...] = src[pl.ds(give, half), :, cols].astype(BF16)
        c = pltpu.make_async_remote_copy(
            src_ref=sends[i], dst_ref=recvs[i], send_sem=w_send.at[i], recv_sem=w_recv.at[i],
            device_id=partner(axis, bit), device_id_type=MESH,
        )
        c.start()
        copies[p, s] = c
        lows[p], sizes[p] = keep, half

    def absorb(p, s):
        copies[p, s].wait()
        i = p * len(stages[p]) + s
        cols = slice(p * step, (p + 1) * step)
        at = pl.ds(lows[p], sizes[p])
        src = acc_in if s == 0 else acc
        total = src[at, :, cols] + recvs[i][...].astype(F32)
        if s + 1 < len(stages[p]):
            acc[at, :, cols] = total
        else:
            half = acc.shape[1] // 2
            up_out[:, cols] = total[0, 0:half]
            down_out[:, cols] = total[0, half:]

    cold_copies, hot_copies = [], []
    for k in range(1, n_table):
        cold_copies.append(pltpu.make_async_remote_copy(
            src_ref=tg_cold.at[table_peer(k)[0]], dst_ref=rc_cold.at[t],
            send_sem=c_send.at[k], recv_sem=c_recv.at[k],
            device_id=table_peer(k), device_id_type=MESH))
        hot_copies.append(pltpu.make_async_remote_copy(
            src_ref=tg_hot.at[:, table_peer(k)[0]], dst_ref=rc_hot.at[t],
            send_sem=h_send.at[k], recv_sem=h_recv.at[k],
            device_id=table_peer(k), device_id_type=MESH))
    for p in range(parts):
        launch(p, 0)
    for c in cold_copies + hot_copies:
        c.start()
    rc_cold[t] = tg_cold[t]
    rc_hot[t] = tg_hot[:, t]
    own_ids[...] = ask_ref[:, :, 0, :]
    for p in range(parts):
        absorb(p, 0)
        launch(p, 1)
    for c in cold_copies + hot_copies:
        c.wait()
    own_cold[...] = rc_cold[...]
    hot_sum = rc_hot[0].astype(F32)
    for o in range(1, n_table):
        hot_sum = hot_sum + rc_hot[o].astype(F32)
    own_hot[...] = hot_sum
    back = []
    for k in range(1, n_rep):
        for n, (src, dst) in enumerate(
            ((own_cold, ag_cold), (own_hot, ag_hot), (own_ids, ag_ids))
        ):
            back.append(pltpu.make_async_remote_copy(
                src_ref=src, dst_ref=dst.at[r], send_sem=a_send.at[n, k],
                recv_sem=a_recv.at[n, k], device_id=rep_peer(k), device_id_type=MESH))
    for c in back:
        c.start()
    ag_cold[r] = own_cold[...]
    ag_hot[r] = own_hot[...]
    ag_ids[r] = own_ids[...]
    deep = len(stages[0])
    for s in range(1, deep):
        for p in range(parts):
            absorb(p, s)
            if s + 1 < deep:
                launch(p, s + 1)
        if s == min(2, deep - 1):
            for c in back:
                c.wait()
            mine = table_out.shape[0]
            first = r * mine
            wants = own_ids.shape[1]
            total = [jnp.zeros((BLOCK, EMB), F32) for _ in range(mine)]
            for q in range(n_rep):
                for o in range(n_table):
                    for w in range(wants):
                        ids = ag_ids[q, o, w:w + 1, :] - first
                        val = ag_cold[q, o, w].astype(F32)
                        for b in range(mine):
                            total[b] = total[b] + jnp.where(ids == b, val, 0.0)
            for h in range(hot_ref.shape[0]):
                ids = hot_ref[h, 0:1, :] - first
                live = hot_ref[h, 0:1, :] >= 0
                val = ag_hot[0, h]
                for q in range(1, n_rep):
                    val = val + ag_hot[q, h]
                for b in range(mine):
                    total[b] = total[b] + jnp.where((ids == b) & live, val, 0.0)
            for b in range(mine):
                table_out[b] = total[b]


def reduce(stages, n_table, n_rep, block_total, acc, tg_cold, tg_hot, ask, hot_ids):
    devices, two, width = acc.shape
    parts = len(stages)
    step = width // parts
    slots, wants = hot_ids.shape[0], tg_cold.shape[1]
    shapes = []
    for part in stages:
        size = devices
        for _ in part:
            size //= 2
            shapes.append(pltpu.VMEM((size, two, step), BF16))
    dma = pltpu.SemaphoreType.DMA
    return pl.pallas_call(
        functools.partial(reduce_kernel, stages, n_table, n_rep, len(shapes)),
        out_shape=[
            jax.ShapeDtypeStruct((two // 2, width), F32),
            jax.ShapeDtypeStruct((two // 2, width), F32),
            jax.ShapeDtypeStruct((block_total // n_rep, BLOCK, EMB), F32),
        ],
        in_specs=vmem(5),
        out_specs=vmem(3),
        scratch_shapes=[
            pltpu.VMEM(acc.shape, F32),
            pltpu.VMEM((n_table, wants, BLOCK, EMB), BF16),
            pltpu.VMEM((n_table, slots, BLOCK, EMB), BF16),
            pltpu.VMEM((n_table, wants, BLOCK, EMB), BF16),
            pltpu.VMEM((slots, BLOCK, EMB), F32),
            pltpu.VMEM((n_rep, n_table, wants, BLOCK, EMB), BF16),
            pltpu.VMEM((n_rep, slots, BLOCK, EMB), F32),
            pltpu.VMEM((n_table, wants, LANES), jnp.int32),
            pltpu.VMEM((n_rep, n_table, wants, LANES), jnp.int32),
        ] + shapes + shapes + [
            dma((len(shapes),)), dma((len(shapes),)),
            dma((n_table,)), dma((n_table,)), dma((n_table,)), dma((n_table,)),
            dma((3, n_rep)), dma((3, n_rep)),
        ],
        compiler_params=pltpu.CompilerParams(collective_id=1, has_side_effects=True),
        name="reduce",
    )(acc, tg_cold, tg_hot, ask, hot_ids)


def make_stages(n_table, n_rep, parts):
    rep = [("replica", b) for b in range(n_rep.bit_length() - 1)]
    tab = [("table", b) for b in range(n_table.bit_length() - 1)]
    bits = rep + tab
    head, tail = bits[:1], bits[1:]
    return [head + tail[p % len(tail):] + tail[:p % len(tail)] for p in range(parts)]


def places(stages, n_rep, devices):
    plan = []
    for part in stages:
        row = []
        for d in range(devices):
            at = 0
            for axis, bit in part:
                number = d // n_rep if axis == "table" else d % n_rep
                at = at * 2 + (number >> bit) % 2
            row.append(at)
        plan.append(row)
    return plan


def fast_local(
    emb_table, cross_up, cross_down, cross_bias, out_weight, bottom_weight, bottom_bias,
    dense_in, labels, lookup_ids, bag_weight, bag_length, want_blocks, hot_blocks, hot_count,
):
    owners, reps = lax.axis_size("table"), lax.axis_size("replica")
    devices = owners * reps
    wants, slots = want_blocks.shape[3], hot_blocks.shape[1]
    want = jnp.broadcast_to(
        want_blocks.reshape(owners, wants)[:, :, None, None], (owners, wants, SUBLANES, LANES)
    )
    alive = jnp.arange(slots, dtype=jnp.int32) < hot_count[0]
    hot_ids = jnp.broadcast_to(
        jnp.where(alive, hot_blocks[0], -1)[:, None, None], (slots, SUBLANES, LANES)
    )
    cold, hot, ask = fetch(want, hot_ids, emb_table, owners)
    parts = 3
    stages = make_stages(owners, reps, parts)
    plan = places(stages, reps, devices)
    acc, cold_grad, hot_grad = compute(
        plan, devices, cold.reshape(-1, EMB), hot.reshape(-1, EMB),
        lookup_ids.transpose(1, 2, 0), bag_weight.transpose(1, 2, 0), bag_length.T,
        dense_in.T, labels[None],
        cross_up, cross_down, cross_bias[None], out_weight[None], bottom_weight,
        bottom_bias[None],
    )
    up, down, table = reduce(
        stages, owners, reps, emb_table.shape[0] // BLOCK, acc, cold_grad.reshape(cold.shape),
        hot_grad.reshape(hot.shape), ask, hot_ids,
    )
    return up, down, table.reshape(-1, EMB)


def local_step(
    cached_rows,
    dense_dev,
    labels_dev,
    ids_dev,
    weight_dev,
    length_dev,
    cross_up,
    cross_down,
    cross_bias,
    out_weight,
    bottom_weight,
    bottom_bias,
):
    batch = ids_dev.shape[0]
    width = cached_rows.shape[1]
    gathered = cached_rows[ids_dev].astype(jnp.float32)
    slots = jnp.arange(ids_dev.shape[2], dtype=jnp.int32)
    bag_coef = jnp.where(
        slots[None, None, :] < length_dev[:, :, None], weight_dev, jnp.zeros((), jnp.float32)
    )
    pooled = jnp.sum(bag_coef[..., None] * gathered, axis=2)
    bottom = jax.nn.relu(
        jnp.dot(dense_dev, bottom_weight, precision=lax.Precision.HIGHEST) + bottom_bias
    )
    cross_base = jnp.concatenate([bottom, pooled.reshape(batch, -1)], 1).astype(jnp.bfloat16)
    low_rank = lax.dot_general(
        cross_base, cross_down, (((1,), (1,)), ((), ())), preferred_element_type=jnp.float32
    ).astype(jnp.bfloat16)
    cross_gate = jnp.dot(low_rank, cross_up, preferred_element_type=jnp.float32) + cross_bias
    base_wide = cross_base.astype(jnp.float32)
    crossed = base_wide * cross_gate + base_wide
    logits = jnp.dot(crossed, out_weight, precision=lax.Precision.HIGHEST)
    logit_grad = jax.nn.sigmoid(logits) - labels_dev.astype(jnp.float32)
    grad_crossed = logit_grad[:, None] * out_weight[None, :]
    g_cross = (grad_crossed * base_wide).astype(jnp.bfloat16)
    g_low = lax.dot_general(
        g_cross, cross_up, (((1,), (1,)), ((), ())), preferred_element_type=jnp.float32
    ).astype(jnp.bfloat16)
    up_part = lax.dot_general(
        low_rank, g_cross, (((0,), (0,)), ((), ())), preferred_element_type=jnp.float32
    )
    down_part = lax.dot_general(
        g_low, cross_base, (((0,), (0,)), ((), ())), preferred_element_type=jnp.float32
    )
    grad_base = grad_crossed * (cross_gate + 1.0) + jnp.dot(
        g_low, cross_down, preferred_element_type=jnp.float32
    )
    grad_pooled = grad_base[:, width:].reshape(batch, -1, width)
    contrib = bag_coef[..., None] * grad_pooled[:, :, None, :]
    cache_grad = (
        jnp.zeros(cached_rows.shape, jnp.float32)
        .at[ids_dev.reshape(-1)]
        .add(contrib.reshape(-1, width))
    )
    return (up_part, down_part, cache_grad)


def plain_local(
    emb_table,
    cross_up,
    cross_down,
    cross_bias,
    out_weight,
    bottom_weight,
    bottom_bias,
    dense_in,
    labels,
    lookup_ids,
    bag_weight,
    bag_length,
    want_blocks,
    hot_blocks,
    hot_count,
):
    owners = lax.axis_size("table")
    blocks = emb_table.reshape(-1, BLOCK, EMB)
    block_total = blocks.shape[0]
    wanted = want_blocks.reshape(owners, want_blocks.shape[3])
    asked_for = lax.all_to_all(wanted, "table", split_axis=0, concat_axis=0, tiled=True)
    served = blocks[asked_for]
    cold_rows = lax.all_to_all(served, "table", split_axis=0, concat_axis=0, tiled=True)
    slot_count = hot_blocks.shape[1]
    alive = jnp.arange(slot_count, dtype=jnp.int32) < hot_count[0]
    own_hot = jnp.where(alive[:, None, None], blocks[hot_blocks[0]], jnp.zeros((), jnp.bfloat16))
    hot_rows = lax.all_gather(own_hot[:, None], "table", axis=1, tiled=True)
    cold_count = cold_rows.shape[0] * cold_rows.shape[1] * BLOCK
    cached_rows = jnp.concatenate([cold_rows.reshape(-1, EMB), hot_rows.reshape(-1, EMB)], 0)
    up_part, down_part, cache_grad = local_step(
        cached_rows,
        dense_in,
        labels,
        lookup_ids,
        bag_weight,
        bag_length,
        cross_up,
        cross_down,
        cross_bias,
        out_weight,
        bottom_weight,
        bottom_bias,
    )
    cold_grad = cache_grad[:cold_count].reshape(cold_rows.shape).astype(jnp.bfloat16)
    returned = lax.all_to_all(cold_grad, "table", split_axis=0, concat_axis=0, tiled=True)
    hot_grad = cache_grad[cold_count:].reshape(hot_rows.shape)
    hot_sums = lax.psum_scatter(hot_grad, "table", scatter_dimension=1, tiled=True)[:, 0]
    block_ids = jnp.arange(block_total, dtype=jnp.int32)
    cold_pick = (asked_for.reshape(-1)[:, None] == block_ids[None, :]).astype(jnp.bfloat16)
    hot_pick = ((hot_blocks[0][:, None] == block_ids[None, :]) & alive[:, None]).astype(jnp.float32)
    block_grad = lax.dot_general(
        cold_pick,
        returned.reshape(cold_pick.shape[0], -1),
        (((0,), (0,)), ((), ())),
        preferred_element_type=jnp.float32,
    )
    block_grad = block_grad + lax.dot_general(
        hot_pick,
        hot_sums.reshape(slot_count, -1),
        (((0,), (0,)), ((), ())),
        precision=lax.Precision.HIGHEST,
    )
    table_grad = lax.psum_scatter(
        block_grad.reshape(-1, EMB), "replica", scatter_dimension=0, tiled=True
    )
    up_grad, down_grad = (
        lax.psum_scatter(up_part, ("table", "replica"), scatter_dimension=0, tiled=True),
        lax.psum_scatter(down_part, ("table", "replica"), scatter_dimension=0, tiled=True),
    )
    return (up_grad, down_grad, table_grad)


def choose(mesh, *args):
    devices = mesh.shape["table"] * mesh.shape["replica"]
    powers = all(n > 1 and n & (n - 1) == 0 for n in mesh.shape.values())
    rank, width = args[1].shape
    ids, want, hot = args[9], args[12], args[13]
    cache = mesh.shape["table"] * (want.shape[3] + hot.shape[1]) * BLOCK
    picked = 2 * ids.shape[0] * ids.shape[1] * cache
    whole_tiles = rank % (devices * SUBLANES) == 0 and width % (3 * LANES) == 0
    if powers and whole_tiles and picked < 2**23:
        return fast_local(*args)
    return plain_local(*args)


def solution(mesh):
    local = functools.partial(choose, mesh)
    placed = (
        P("table", None),
        P(),
        P(),
        P(),
        P(),
        P(),
        P(),
        P(("table", "replica"), None),
        P(("table", "replica")),
        P(("table", "replica"), None, None),
        P(("table", "replica"), None, None),
        P(("table", "replica"), None),
        P("table", "replica", None, None),
        P("table", None),
        P("table"),
    )
    return jax.shard_map(
        local,
        mesh=mesh,
        in_specs=placed,
        out_specs=(
            P(("table", "replica"), None),
            P(("table", "replica"), None),
            P(("table", "replica"), None),
        ),
        check_vma=False,
    )
```
